32 devices in a mesh: row: 8 (over y, x, core), col: 4 (over z).
Axes of the slice: x: 2, y: 2, z: 4, core: 2. Of those that a mesh axis runs over, the one named last changes fastest.
Arguments:
- object_slices: float32 [2, 2, 1024, 512], P(None, None, 'row', 'col'), may hold values from -4 to 4
- probe: float32 [2, 128, 128], replicated, may hold values from -5 to 5
- phase: float32 [128, 128], replicated, may hold values from -3.140625 to 3.140625
- positions: int32 [8, 4, 4, 2], P('row', 'col'), may hold values from 0 to 127
- counts: int32 [8, 4], P('row', 'col'), may hold values from 1 to 4
- measured: float32 [8, 4, 4, 128, 128], P('row', 'col'), may hold values from 0.2 to 4
Outputs:
- updated: float32 [2, 2, 1024, 512], P(None, None, 'row', 'col')
The draws below stay inside these ranges and needn't reach their ends.
Inputs may be any that keep to these rules, and one draw needn't show every extreme that they name: Slots k with k >= counts of the tile are padding and do not contribute. `positions`: a window may reach up to 127 pixels into the tiles below, to the right and diagonally below right.
All inputs are finite; a program needn't handle non-finite values.
Results may differ from the reference program's by a relative error of at most 0.0003.
Values sent between devices are 32-bit elements; how exact they have to be, the bound alone decides.
No kernel may reach another device: no remote copies, remote signals or barrier semaphores. Data moves between devices by JAX's collectives and lax.ppermute only.
A program may use at most 64 MiB of HBM per device.

```python
import math
import jax
import jax.numpy as jnp
from jax import lax

TILE = 128
WINDOW_PIXELS = 128
PROBE_SLOTS = 4
SLICES = 2
ITERS = 2
NR = 1024
NC = 512
N_ROW = 8
N_COL = 4


def touch_ends(entries, stream_key, least, top_value):
    dims = entries.shape
    place = [jax.random.randint(jax.random.fold_in(stream_key, axis), (), 0, dims[axis]) for axis in range(len(dims))]
    entries = entries.at[tuple(place)].set(least)
    longest = dims.index(max(dims))
    place[longest] = (place[longest] + 1) % dims[longest]
    return entries.at[tuple(place)].set(top_value)


def block_scale(rng, dims, pieces, low, high):
    gain, own = 1.0, jax.random.fold_in(rng, 6)
    for axis_at, shards_of in pieces:
        draws = jnp.exp(jax.random.uniform(jax.random.fold_in(own, axis_at), (shards_of,), jnp.float32, low / len(pieces), high / len(pieces)))
        gain = gain * jnp.repeat(draws, dims[axis_at] // shards_of).reshape([-1 if axis == axis_at else 1 for axis in range(len(dims))])
    return gain


def bell_draw(key, dims, scale, most, cuts=(), kind=jnp.bfloat16):
    gain = block_scale(key, dims, cuts, -0.22, 0.18) if cuts else 1.0
    drawn = jax.random.normal(key, dims, jnp.float32) * scale * gain
    return jnp.minimum(jnp.maximum(drawn, -most), most).astype(kind)


def setup_inputs(seed: int = 0) -> dict:
    keys = jax.random.split(jax.random.key(seed), 7)
    object_slices = bell_draw(keys[0], (SLICES, 2, NR, NC), 0.7, 4.0, ((2, 8), (3, 4)), jnp.float32)
    probe = bell_draw(keys[1], (2, WINDOW_PIXELS, WINDOW_PIXELS), 1.0, 5.0, (), jnp.float32)
    phase = jnp.clip(jax.random.uniform(keys[2], (WINDOW_PIXELS, WINDOW_PIXELS), jnp.float32, -3.140625, 3.140625), -3.140625, 3.140625)
    positions = touch_ends(jax.random.randint(keys[3], (N_ROW, N_COL, PROBE_SLOTS, 2), 0, TILE), jax.random.fold_in(keys[3], 1), 0, TILE - 1).astype(jnp.int32)
    counts = touch_ends(jax.random.randint(keys[4], (N_ROW, N_COL), 1, PROBE_SLOTS + 1), jax.random.fold_in(keys[4], 1), 1, PROBE_SLOTS).astype(jnp.int32)
    measured = jnp.clip(jnp.exp(math.log(4.0) - 2.9957323 * jax.random.uniform(keys[5], (N_ROW, N_COL, PROBE_SLOTS, WINDOW_PIXELS, WINDOW_PIXELS), jnp.float32) ** block_scale(keys[5], (N_ROW, N_COL, PROBE_SLOTS, WINDOW_PIXELS, WINDOW_PIXELS), ((0, 8), (1, 4)), -0.2, 0.2)), 0.2, 4.0)
    return dict(object_slices=object_slices, probe=probe, phase=phase, positions=positions, counts=counts, measured=measured)


step_rate = 0.02

def dft_tables(width):
    index = jnp.arange(width, dtype=jnp.int32)
    product = index[:, None] * index[None, :] % width
    angle = product.astype(jnp.float32) * (-2.0 * jnp.pi / width)
    scale = 1.0 / jnp.sqrt(jnp.float32(width))
    return (jnp.cos(angle) * scale, jnp.sin(angle) * scale)

def transform(real, imag, table_re, table_im):
    high = lax.Precision.HIGHEST
    left_re = jnp.einsum('ij,njk->nik', table_re, real, precision=high) - jnp.einsum('ij,njk->nik', table_im, imag, precision=high)
    left_im = jnp.einsum('ij,njk->nik', table_re, imag, precision=high) + jnp.einsum('ij,njk->nik', table_im, real, precision=high)
    out_re = jnp.einsum('nij,jk->nik', left_re, table_re, precision=high) - jnp.einsum('nij,jk->nik', left_im, table_im, precision=high)
    out_im = jnp.einsum('nij,jk->nik', left_re, table_im, precision=high) + jnp.einsum('nij,jk->nik', left_im, table_re, precision=high)
    return (out_re, out_im)

def local_loss(extended, positions, live, probe, phase, measured):
    width = probe.shape[-1]
    layers = extended.shape[0]
    table_re, table_im = dft_tables(width)

    def window(corner):
        corner = corner.astype(jnp.int32)
        zero = jnp.zeros((), jnp.int32)
        return lax.dynamic_slice(extended, (zero, zero, corner[0], corner[1]), (layers, 2, width, width))
    windows = jax.vmap(window)(positions)
    wave_re = jnp.broadcast_to(probe[0], windows[:, 0, 0].shape)
    wave_im = jnp.broadcast_to(probe[1], windows[:, 0, 0].shape)
    prop_re = jnp.cos(phase)
    prop_im = jnp.sin(phase)
    for layer in range(layers):
        obj_re = windows[:, layer, 0]
        obj_im = windows[:, layer, 1]
        wave_re, wave_im = (wave_re * obj_re - wave_im * obj_im, wave_re * obj_im + wave_im * obj_re)
        if layer + 1 < layers:
            spec_re, spec_im = transform(wave_re, wave_im, table_re, table_im)
            spec_re, spec_im = (spec_re * prop_re - spec_im * prop_im, spec_re * prop_im + spec_im * prop_re)
            wave_re, wave_im = transform(spec_re, spec_im, table_re, -table_im)
    far_re, far_im = transform(wave_re, wave_im, table_re, table_im)
    misfit = far_re * far_re + far_im * far_im - measured
    return 0.5 * jnp.sum(live[:, None, None] * misfit * misfit)

def tile_gradient(extended, positions, count, measured, probe, phase):
    slots = positions.shape[0]
    live = (jnp.arange(slots, dtype=jnp.int32) < count).astype(jnp.float32)
    loss, pull = jax.vjp(lambda e: local_loss(e, positions, live, probe, phase, measured), extended)
    return pull(jnp.ones_like(loss))[0]

def reference(object_slices, probe, phase, positions, counts, measured):
    tiles = object_slices.reshape(SLICES, 2, N_ROW, TILE, N_COL, TILE).transpose(2, 4, 0, 1, 3, 5)
    edge = TILE + WINDOW_PIXELS
    flattened_positions = positions.reshape(N_ROW * N_COL, PROBE_SLOTS, 2)
    flattened_counts = counts.reshape(N_ROW * N_COL)
    flattened_measurements = measured.reshape(N_ROW * N_COL, PROBE_SLOTS, WINDOW_PIXELS, WINDOW_PIXELS)
    for step in range(ITERS):
        right = jnp.roll(tiles, -1, axis=1)[..., :WINDOW_PIXELS]
        wide = jnp.concatenate([tiles, right], axis=-1)
        below = jnp.roll(wide, -1, axis=0)[..., :WINDOW_PIXELS, :]
        extended = jnp.concatenate([wide, below], axis=-2)
        flattened_extended = extended.reshape(N_ROW * N_COL, SLICES, 2, edge, edge)
        gradient_list = lax.map(lambda element: tile_gradient(element[0], element[1], element[2], element[3], probe, phase), (flattened_extended, flattened_positions, flattened_counts, flattened_measurements))
        gradient_list = gradient_list.reshape(N_ROW, N_COL, SLICES, 2, edge, edge)
        bottom = gradient_list[..., TILE:, :]
        upper = gradient_list[..., :TILE, :].at[..., :WINDOW_PIXELS, :].add(jnp.roll(bottom, 1, axis=0))
        side = upper[..., TILE:]
        owned = upper[..., :TILE].at[..., :WINDOW_PIXELS].add(jnp.roll(side, 1, axis=1))
        tiles = tiles - step_rate * owned
    return tiles.transpose(2, 3, 0, 4, 1, 5).reshape(SLICES, 2, N_ROW * TILE, N_COL * TILE)
```

```python
import functools

import jax
import jax.numpy as jnp
import ml_dtypes
import numpy as np
from jax import lax
from jax.experimental import pallas as pl
from jax.experimental.pallas import tpu as pltpu
from jax.sharding import PartitionSpec as P

ITERS = 2
step_rate = 0.02
F32 = jnp.float32
BF16 = jnp.bfloat16
VMEM = pl.BlockSpec(memory_space=pltpu.VMEM)
SMEM = pl.BlockSpec(memory_space=pltpu.SMEM)


def moved(value, rows, cols):
    nr, nc = lax.axis_size("row"), lax.axis_size("col")
    pairs = [
        (r * nc + c, ((r + rows) % nr) * nc + (c + cols) % nc)
        for r in range(nr)
        for c in range(nc)
    ]
    return lax.ppermute(value, ("row", "col"), pairs)


def dft_tables(width):
    index = np.arange(width)
    angle = (index[:, None] * index[None, :] % width) * (-2.0 * np.pi / width)
    cos, sin = np.cos(angle) / np.sqrt(width), np.sin(angle) / np.sqrt(width)
    right = np.block([[cos, sin], [-sin, cos]]).astype(np.float32)
    left = np.block([[cos, -sin], [sin, cos]]).astype(np.float32)
    tables = []
    for table in (right, left):
        high = table.astype(ml_dtypes.bfloat16)
        low = (table - high.astype(np.float32)).astype(ml_dtypes.bfloat16)
        tables += [high, low]
    return [jnp.asarray(t) for t in tables]


def halves(x):
    high = x.astype(BF16)
    low = (x - high.astype(F32)).astype(BF16)
    return high, low


def dot3(a, b):
    (ah, al), (bh, bl) = a, b
    mm = functools.partial(jnp.dot, preferred_element_type=F32)
    return mm(ah, bh) + mm(al, bh) + mm(ah, bl)


def along_lanes(z, table):
    n = z[0][0].shape[0]
    x = jnp.concatenate([jnp.concatenate(s, axis=1) for s in z], axis=0)
    y = dot3(halves(x), table)
    return [(y[k * n : (k + 1) * n, :n], y[k * n : (k + 1) * n, n:]) for k in range(2)]


def along_rows(z, table):
    n = z[0][0].shape[0]
    x = jnp.concatenate(
        [jnp.concatenate([s[part] for s in z], axis=1) for part in range(2)], axis=0
    )
    y = dot3(table, halves(x))
    return [(y[:n, k * n : (k + 1) * n], y[n:, k * n : (k + 1) * n]) for k in range(2)]


def times(a, b):
    return (a[0] * b[0] - a[1] * b[1], a[0] * b[1] + a[1] * b[0])


def times_conj(a, b):
    return (a[0] * b[0] + a[1] * b[1], a[1] * b[0] - a[0] * b[1])


def own_masks(positions, slot, width):
    rows = lax.broadcasted_iota(jnp.int32, (width, width), 0)
    cols = lax.broadcasted_iota(jnp.int32, (width, width), 1)
    return rows >= positions[2 * slot], cols >= positions[2 * slot + 1]


def window(tiles, masks, part):
    t00, t01, t10, t11 = (t[part] for t in tiles)
    rm, cm = masks
    return jnp.where(rm, jnp.where(cm, t00, t01), jnp.where(cm, t10, t11))


def scatter(outs, masks, g, first):
    rm, cm = masks
    for part in range(2):
        top = jnp.where(rm, g[part], 0.0)
        low = jnp.where(rm, 0.0, g[part])
        for ref, value in zip(
            outs,
            (
                jnp.where(cm, top, 0.0),
                jnp.where(cm, 0.0, top),
                jnp.where(cm, low, 0.0),
                jnp.where(cm, 0.0, low),
            ),
        ):
            if first:
                ref[part] = value
            else:
                ref[part] += value


def prepare_kernel(positions, probe, phase, rolled, prop):
    for slot in range(rolled.shape[0]):
        for part in range(2):
            x = pltpu.roll(probe[part], positions[2 * slot], 0)
            rolled[slot, part] = pltpu.roll(x, positions[2 * slot + 1], 1)
    prop[0] = jnp.cos(phase[...])
    prop[1] = jnp.sin(phase[...])


def first_slice_kernel(positions, rolled, t00, t01, t10, t11, prop, rh, rl, lh, ll, wave):
    right, left = (rh[...], rl[...]), (lh[...], ll[...])
    width = prop.shape[-1]
    tiles = (t00, t01, t10, t11)
    h = (prop[0], prop[1])
    for pair in range(0, rolled.shape[0], 2):
        z = []
        for slot in (pair, pair + 1):
            masks = own_masks(positions, slot, width)
            w = [window(tiles, masks, part) for part in range(2)]
            z.append(times((rolled[slot, 0], rolled[slot, 1]), w))
        z = along_rows(along_lanes(z, right), left)
        z = [times(s, h) for s in z]
        z = along_lanes(along_rows(z, right), left)
        for k in range(2):
            wave[pair + k, 0], wave[pair + k, 1] = z[k]


def second_slice_kernel(
    positions, counts, wave, t00, t01, t10, t11, measured, rh, rl, lh, ll, g00, g01, g10, g11, back
):
    right, left = (rh[...], rl[...]), (lh[...], ll[...])
    width = measured.shape[-1]
    tiles = (t00, t01, t10, t11)
    for pair in range(0, wave.shape[0], 2):
        z = []
        for slot in (pair, pair + 1):
            masks = own_masks(positions, slot, width)
            w = [window(tiles, masks, part) for part in range(2)]
            z.append(times((wave[slot, 0], wave[slot, 1]), w))
        z = along_rows(along_lanes(z, right), left)
        g = []
        for k in range(2):
            re, im = z[k]
            live = (pair + k < counts[0]).astype(F32)
            pull = (re * re + im * im - measured[pair + k]) * (2.0 * live)
            g.append((pull * re, pull * im))
        g = along_lanes(along_rows(g, right), left)
        for k in range(2):
            slot = pair + k
            masks = own_masks(positions, slot, width)
            w = [window(tiles, masks, part) for part in range(2)]
            scatter(
                (g00, g01, g10, g11),
                masks,
                times_conj(g[k], (wave[slot, 0], wave[slot, 1])),
                slot == 0,
            )
            back[slot, 0], back[slot, 1] = times_conj(g[k], w)


def first_back_kernel(positions, back, rolled, prop, rh, rl, lh, ll, g00, g01, g10, g11):
    right, left = (rh[...], rl[...]), (lh[...], ll[...])
    width = prop.shape[-1]
    h = (prop[0], prop[1])
    for pair in range(0, rolled.shape[0], 2):
        z = [(back[slot, 0], back[slot, 1]) for slot in (pair, pair + 1)]
        z = along_rows(along_lanes(z, right), left)
        z = [times_conj(s, h) for s in z]
        z = along_lanes(along_rows(z, right), left)
        for k in range(2):
            slot = pair + k
            masks = own_masks(positions, slot, width)
            scatter(
                (g00, g01, g10, g11),
                masks,
                times_conj(z[k], (rolled[slot, 0], rolled[slot, 1])),
                slot == 0,
            )


def update_kernel(tile, own, right, below, corner, out):
    out[...] = tile[...] - step_rate * (own[...] + right[...] + below[...] + corner[...])


def call(kernel, ins, outs, args, name):
    return pl.pallas_call(
        kernel,
        out_shape=outs,
        in_specs=ins,
        out_specs=[VMEM] * len(outs) if isinstance(outs, (list, tuple)) else VMEM,
        name=name,
    )(*args)


def per_device(object_slices, probe, phase, positions, counts, measured):
    width = probe.shape[-1]
    assert object_slices.shape[-1] == width and object_slices.shape[-2] == width
    corners = positions.reshape(-1)
    slots = positions.shape[2]
    live = counts.reshape(-1)
    intensity = measured[0, 0]
    tables = dft_tables(width)
    plane = jax.ShapeDtypeStruct((2, width, width), F32)
    stack = jax.ShapeDtypeStruct((slots, 2, width, width), F32)

    rolled, prop = call(
        prepare_kernel, [SMEM, VMEM, VMEM], [stack, plane], (corners, probe, phase), "prepare"
    )

    def fetch(tile):
        return tile, moved(tile, 0, -1), moved(tile, -1, 0), moved(tile, -1, -1)

    def returned(g):
        return g[0], moved(g[1], 0, 1), moved(g[2], 1, 0), moved(g[3], 1, 1)

    def update(tile, g):
        return call(update_kernel, [VMEM] * 5, plane, (tile, *g), "update")

    first, second = object_slices[0], object_slices[1]
    for _ in range(ITERS):
        tiles0 = fetch(first)
        tiles1 = fetch(second)
        wave = call(
            first_slice_kernel,
            [SMEM] + [VMEM] * 10,
            stack,
            (corners, rolled, *tiles0, prop, *tables),
            "first",
        )
        *g1, back = call(
            second_slice_kernel,
            [SMEM] * 2 + [VMEM] * 10,
            [plane] * 4 + [stack],
            (corners, live, wave, *tiles1, intensity, *tables),
            "second",
        )
        g1 = returned(g1)
        g0 = call(
            first_back_kernel,
            [SMEM] + [VMEM] * 7,
            [plane] * 4,
            (corners, back, rolled, prop, *tables),
            "back",
        )
        g0 = returned(g0)
        second = update(second, g1)
        first = update(first, g0)
    return jnp.stack([first, second])


def solution(mesh):
    return jax.shard_map(
        per_device,
        mesh=mesh,
        in_specs=(
            P(None, None, "row", "col"),
            P(),
            P(),
            P("row", "col", None, None),
            P("row", "col"),
            P("row", "col", None, None, None),
        ),
        out_specs=P(None, None, "row", "col"),
        check_vma=False,
    )
```

```python
import functools

import jax
import jax.numpy as jnp
import ml_dtypes
import numpy as np
from jax import lax
from jax.experimental import pallas as pl
from jax.experimental.pallas import tpu as pltpu
from jax.sharding import PartitionSpec as P

ITERS = 2
VLIM = 24 * 2**20
FUSED = True
step_rate = 0.02
F32 = jnp.float32
BF16 = jnp.bfloat16
VMEM = pl.BlockSpec(memory_space=pltpu.VMEM)
SMEM = pl.BlockSpec(memory_space=pltpu.SMEM)


def moved(value, rows, cols, parity=None):
    nr, nc = lax.axis_size("row"), lax.axis_size("col")
    pairs = [
        (r * nc + c, ((r + rows) % nr) * nc + (c + cols) % nc)
        for r in range(nr)
        for c in range(nc)
        if parity is None or r % 2 == parity
    ]
    return lax.ppermute(value, ("row", "col"), pairs)


def dft_tables(width):
    index = np.arange(width)
    angle = (index[:, None] * index[None, :] % width) * (-2.0 * np.pi / width)
    cos, sin = np.cos(angle) / np.sqrt(width), np.sin(angle) / np.sqrt(width)
    right = np.block([[cos, sin], [-sin, cos]]).astype(np.float32)
    left = np.block([[cos, -sin], [sin, cos]]).astype(np.float32)
    tables = []
    for table in (right, left):
        high = table.astype(ml_dtypes.bfloat16)
        low = (table - high.astype(np.float32)).astype(ml_dtypes.bfloat16)
        tables += [high, low]
    return jnp.asarray(np.stack(tables))


def halves(x):
    high = x.astype(BF16)
    low = (x - high.astype(F32)).astype(BF16)
    return high, low


def dot3(a, b):
    (ah, al), (bh, bl) = a, b
    mm = functools.partial(jnp.dot, preferred_element_type=F32)
    return mm(ah, bh) + mm(al, bh) + mm(ah, bl)


def along_lanes(z, table):
    n = z[0][0].shape[0]
    x = jnp.concatenate([jnp.concatenate(s, axis=1) for s in z], axis=0)
    y = dot3(halves(x), table)
    return [(y[k * n : (k + 1) * n, :n], y[k * n : (k + 1) * n, n:]) for k in range(2)]


def along_rows(z, table):
    n = z[0][0].shape[0]
    x = jnp.concatenate(
        [jnp.concatenate([s[part] for s in z], axis=1) for part in range(2)], axis=0
    )
    y = dot3(table, halves(x))
    return [(y[:n, k * n : (k + 1) * n], y[n:, k * n : (k + 1) * n]) for k in range(2)]


def times(a, b):
    return (a[0] * b[0] - a[1] * b[1], a[0] * b[1] + a[1] * b[0])


def times_conj(a, b):
    return (a[0] * b[0] + a[1] * b[1], a[1] * b[0] - a[0] * b[1])


def own_masks(positions, slot, width):
    rows = lax.broadcasted_iota(jnp.int32, (width, width), 0)
    cols = lax.broadcasted_iota(jnp.int32, (width, width), 1)
    return rows >= positions[2 * slot], cols >= positions[2 * slot + 1]


def window(tiles, masks, part):
    t00, t01, t10, t11 = (t[part] for t in tiles)
    rm, cm = masks
    return jnp.where(rm, jnp.where(cm, t00, t01), jnp.where(cm, t10, t11))


def scatter(outs, masks, g, first):
    rm, cm = masks
    for part in range(2):
        top = jnp.where(rm, g[part], 0.0)
        low = jnp.where(rm, 0.0, g[part])
        for ref, value in zip(
            outs,
            (
                jnp.where(cm, top, 0.0),
                jnp.where(cm, 0.0, top),
                jnp.where(cm, low, 0.0),
                jnp.where(cm, 0.0, low),
            ),
        ):
            if first:
                ref[part] = value
            else:
                ref[part] += value


def prepare_kernel(positions, probe, phase, measured, constants, rolled, prop, intensity, tables):
    tables[...] = constants[...]
    intensity[...] = measured[...]
    for slot in range(rolled.shape[0]):
        for part in range(2):
            x = pltpu.roll(probe[part], positions[2 * slot], 0)
            rolled[slot, part] = pltpu.roll(x, positions[2 * slot + 1], 1)
    prop[0] = jnp.cos(phase[...])
    prop[1] = jnp.sin(phase[...])


def first_slice_kernel(positions, rolled, t00, t01, t10, t11, prop, tables, wave):
    right, left = (tables[0], tables[1]), (tables[2], tables[3])
    width = prop.shape[-1]
    tiles = (t00, t01, t10, t11)
    h = (prop[0], prop[1])
    for pair in range(0, rolled.shape[0], 2):
        z = []
        for slot in (pair, pair + 1):
            masks = own_masks(positions, slot, width)
            w = [window(tiles, masks, part) for part in range(2)]
            z.append(times((rolled[slot, 0], rolled[slot, 1]), w))
        z = along_rows(along_lanes(z, right), left)
        z = [times(s, h) for s in z]
        z = along_lanes(along_rows(z, right), left)
        for k in range(2):
            wave[pair + k, 0], wave[pair + k, 1] = z[k]


def second_slice_kernel(
    positions, counts, wave, t00, t01, t10, t11, measured, tables, g00, g01, g10, g11, back
):
    right, left = (tables[0], tables[1]), (tables[2], tables[3])
    width = measured.shape[-1]
    tiles = (t00, t01, t10, t11)
    for pair in range(0, wave.shape[0], 2):
        z = []
        for slot in (pair, pair + 1):
            masks = own_masks(positions, slot, width)
            w = [window(tiles, masks, part) for part in range(2)]
            z.append(times((wave[slot, 0], wave[slot, 1]), w))
        z = along_rows(along_lanes(z, right), left)
        g = []
        for k in range(2):
            re, im = z[k]
            live = (pair + k < counts[0]).astype(F32)
            pull = (re * re + im * im - measured[pair + k]) * (2.0 * live)
            g.append((pull * re, pull * im))
        g = along_lanes(along_rows(g, right), left)
        for k in range(2):
            slot = pair + k
            masks = own_masks(positions, slot, width)
            w = [window(tiles, masks, part) for part in range(2)]
            scatter(
                (g00, g01, g10, g11),
                masks,
                times_conj(g[k], (wave[slot, 0], wave[slot, 1])),
                slot == 0,
            )
            back[slot, 0], back[slot, 1] = times_conj(g[k], w)


def first_back_kernel(positions, back, rolled, prop, tables, g00, g01, g10, g11):
    right, left = (tables[0], tables[1]), (tables[2], tables[3])
    width = prop.shape[-1]
    h = (prop[0], prop[1])
    for pair in range(0, rolled.shape[0], 2):
        z = [(back[slot, 0], back[slot, 1]) for slot in (pair, pair + 1)]
        z = along_rows(along_lanes(z, right), left)
        z = [times_conj(s, h) for s in z]
        z = along_lanes(along_rows(z, right), left)
        for k in range(2):
            slot = pair + k
            masks = own_masks(positions, slot, width)
            scatter(
                (g00, g01, g10, g11),
                masks,
                times_conj(z[k], (rolled[slot, 0], rolled[slot, 1])),
                slot == 0,
            )


def add_kernel(a, b, out):
    out[...] = a[...] + b[...]


def update_kernel(tile, own, right, below, out):
    out[...] = tile[...] - step_rate * (own[...] + right[...] + below[...])


def last_kernel(*refs):
    *ins, out = refs
    update_kernel(*ins[:4], out.at[0])
    update_kernel(*ins[4:], out.at[1])


def call(kernel, ins, outs, args, name, scratch=()):
    return pl.pallas_call(
        kernel,
        out_shape=outs,
        in_specs=ins,
        out_specs=[VMEM] * len(outs) if isinstance(outs, (list, tuple)) else VMEM,
        name=name,
        scratch_shapes=scratch,
        compiler_params=pltpu.CompilerParams(vmem_limit_bytes=VLIM),
    )(*args)


def second_back_kernel(
    positions, counts, rolled, prop, wave, t00, t01, t10, t11, measured, tables, g00, g01, g10, g11, h00, h01, h10, h11, back
):
    second_slice_kernel(
        positions, counts, wave, t00, t01, t10, t11, measured, tables, g00, g01, g10, g11, back
    )
    first_back_kernel(positions, back, rolled, prop, tables, h00, h01, h10, h11)


def per_device(object_slices, probe, phase, positions, counts, measured):
    width = probe.shape[-1]
    assert object_slices.shape[-1] == width and object_slices.shape[-2] == width
    corners = positions.reshape(-1)
    slots = positions.shape[2]
    live = counts.reshape(-1)
    intensity = measured[0, 0]
    tables = dft_tables(width)
    plane = jax.ShapeDtypeStruct((2, width, width), F32)
    stack = jax.ShapeDtypeStruct((slots, 2, width, width), F32)
    like = lambda x: jax.ShapeDtypeStruct(x.shape, x.dtype)

    rolled, prop, intensity, tables = call(
        prepare_kernel,
        [SMEM] + [VMEM] * 4,
        [stack, plane, like(intensity), like(tables)],
        (corners, probe, phase, intensity, tables),
        "prepare",
    )

    def fetch(tile, after=None):
        right = moved(tile, 0, -1)
        below = moved(tile, -1, 0)
        if after is not None:
            right, _ = lax.optimization_barrier((right, after))
        return tile, right, below, moved(right, -1, 0)

    def returned(g):
        near = moved(g[3], 1, 0)
        low = moved(g[2], 1, 0)
        side = call(add_kernel, [VMEM] * 2, plane, (g[1], near), "side")
        return g[0], moved(side, 0, 1), low

    first, second = object_slices[0], object_slices[1]
    for step in range(ITERS):
        tiles0 = fetch(first)
        tiles1 = fetch(second, rolled if step == 0 else None)
        wave = call(
            first_slice_kernel,
            [SMEM] + [VMEM] * 7,
            stack,
            (corners, rolled, *tiles0, prop, tables),
            "first",
        )
        if FUSED:
            *g, _ = call(
                second_back_kernel,
                [SMEM] * 2 + [VMEM] * 9,
                [plane] * 8 + [stack],
                (corners, live, rolled, prop, wave, *tiles1, intensity, tables),
                "second_back",
            )
            g1, g0 = g[:4], g[4:]
        else:
            *g1, back = call(
                second_slice_kernel,
                [SMEM] * 2 + [VMEM] * 7,
                [plane] * 4 + [stack],
                (corners, live, wave, *tiles1, intensity, tables),
                "second",
            )
            g0 = call(
                first_back_kernel,
                [SMEM] + [VMEM] * 4,
                [plane] * 4,
                (corners, back, rolled, prop, tables),
                "back",
            )
        g1 = returned(g1)
        g0 = returned(g0)
        if step + 1 < ITERS:
            second = call(update_kernel, [VMEM] * 4, plane, (second, *g1), "update")
            first = call(update_kernel, [VMEM] * 4, plane, (first, *g0), "update")
    return call(
        last_kernel, [VMEM] * 8, like(object_slices), (first, *g0, second, *g1), "last"
    )


def solution(mesh):
    return jax.shard_map(
        per_device,
        mesh=mesh,
        in_specs=(
            P(None, None, "row", "col"),
            P(),
            P(),
            P("row", "col", None, None),
            P("row", "col"),
            P("row", "col", None, None, None),
        ),
        out_specs=P(None, None, "row", "col"),
        check_vma=False,
    )
```
